32 devices in a mesh: samp: 4 (over x, core), bin: 8 (over z, y).
Axes of the slice: x: 2, y: 2, z: 4, core: 2. Of those that a mesh axis runs over, the one named last changes fastest.
Arguments:
- read_depth: bfloat16 [32768, 4096], P('samp', 'bin'), may hold values from -18 to 18
- gc_weight: float32 [4096], replicated, may hold values from 0.3 to 3
- map_weight: float32 [4096], replicated, may hold values from 0.3 to 3
- kernel: float32 [33], replicated, may hold values from 0.2 to 1
- loadings: bfloat16 [20, 4096], P(None, 'bin'), may hold values from -0.09375 to 0.09375
Outputs:
- zscore: bfloat16 [32768, 4096], P(('samp', 'bin'))
- scores: float32 [32768, 20], P(('samp', 'bin'))
The draws below stay inside these ranges and needn't reach their ends.
All inputs are finite; a program needn't handle non-finite values.
Results may differ from the reference program's by a relative error of at most 0.017.
Values may be sent and summed in bfloat16 or wider, within the bound.
A program may use at most 128 MiB of HBM per device.

```python
import math
import jax
import jax.numpy as jnp
from jax import lax

S_DEV = 8192
K = 20
RADIUS = 16
SAMPLES = 32768
BINS = 4096
N_SAMP = 4


def draw_read_depth(key, part):
    offset_key = jax.random.fold_in(key, 11)
    noise_key = jax.random.fold_in(key, 23)
    offsets = jax.random.uniform(offset_key, (BINS,), jnp.float32, -1.5, 1.5)
    noise = jnp.clip(jax.random.normal(noise_key, (SAMPLES, BINS), jnp.float32), -4.0, 4.0)
    rising = 1.0 + 2.0 * jnp.arange(SAMPLES).astype(jnp.float32) / max(SAMPLES - 1, 1)
    values = rising[:, None] * (offsets[None, :] + noise)
    return values.astype(jnp.bfloat16)


def level_of(stream_key, dims, pieces, least, high):
    level, own = 1.0, jax.random.fold_in(stream_key, 6)
    for dim, parts in pieces:
        heights = jnp.exp(jax.random.uniform(jax.random.fold_in(own, dim), (parts,), jnp.float32, least / len(pieces), high / len(pieces)))
        level = level * jnp.repeat(heights, dims[dim] // parts).reshape([-1 if axis == dim else 1 for axis in range(len(dims))])
    return level


def normal_values(stream_key, shape, scale, most, cuts=(), kind=jnp.bfloat16):
    drawn = jax.random.normal(stream_key, shape, jnp.float32) * scale
    if len(cuts) > 0:
        drawn = level_of(stream_key, shape, cuts, -0.22, 0.18) * drawn
    return jnp.clip(drawn, min=-most, max=most).astype(kind)


def setup_inputs(seed: int = 0) -> dict:
    seeds = jax.random.split(jax.random.key(seed), 6)
    read_depth = draw_read_depth(jax.random.fold_in(seeds[5], 71), 0)
    gc_weight = jnp.clip(jnp.exp(jax.random.uniform(seeds[1], (BINS,), jnp.float32, math.log(0.3), math.log(3.0))), 0.3, 3.0)
    map_weight = jnp.clip(jnp.exp(jax.random.uniform(seeds[2], (BINS,), jnp.float32, math.log(0.3), math.log(3.0))), 0.3, 3.0)
    kernel = jnp.clip(jnp.exp(jax.random.uniform(seeds[3], (2 * RADIUS + 1,), jnp.float32, math.log(0.2), math.log(1.0))), 0.2, 1.0)
    loadings = normal_values(seeds[4], (K, BINS), BINS ** -0.5, 0.09375, ((1, 8),))
    return dict(read_depth=read_depth, gc_weight=gc_weight, map_weight=map_weight, kernel=kernel, loadings=loadings)


def smooth(rows_in, weights, kernel):
    bin_count = rows_in.shape[1]
    padded = jnp.pad(rows_in, ((0, 0), (RADIUS, RADIUS)))
    weight_padded = jnp.pad(weights, (RADIUS, RADIUS))
    numerator = jnp.zeros(rows_in.shape, jnp.float32)
    denominator = jnp.zeros((bin_count,), jnp.float32)
    for position in range(2 * RADIUS + 1):
        coefficient = kernel[position] * weight_padded[position:position + bin_count]
        numerator = numerator + coefficient * padded[:, position:position + bin_count].astype(jnp.float32)
        denominator = denominator + coefficient
    return numerator / denominator

def reference(read_depth, gc_weight, map_weight, kernel, loadings):
    weights = gc_weight * map_weight
    groups = read_depth.reshape(N_SAMP, S_DEV, BINS)

    def column_sums(rows_in):
        return lax.optimization_barrier(jnp.sum(smooth(rows_in, weights, kernel), axis=0))
    totals = lax.optimization_barrier(jnp.sum(lax.map(column_sums, groups), axis=0))
    bin_mean = totals / SAMPLES

    def finish(rows_in):
        centred = (smooth(rows_in, weights, kernel) - bin_mean).astype(jnp.bfloat16)
        scores = jnp.dot(centred, loadings.T, preferred_element_type=jnp.float32)
        residual = centred.astype(jnp.float32) - jnp.dot(scores, loadings.astype(jnp.float32), precision=lax.Precision.HIGHEST)
        row_mean = lax.optimization_barrier(jnp.mean(residual, axis=1, keepdims=True))
        shifted = residual - row_mean
        variance = lax.optimization_barrier(jnp.mean(shifted * shifted, axis=1, keepdims=True))
        return ((shifted / jnp.sqrt(variance + 1e-05)).astype(jnp.bfloat16), scores)
    zscore, scores = lax.map(finish, groups)
    return (zscore.reshape(SAMPLES, BINS), scores.reshape(SAMPLES, K))
```

```python
import functools

import jax
import jax.numpy as jnp
from jax import lax
from jax.experimental import pallas as pl
from jax.experimental.pallas import tpu as pltpu
from jax.sharding import PartitionSpec as P

RADIUS = 16
EDGE = 128
OUT = 256
WIN = OUT + 2 * EDGE
CHUNK = 128
AHEAD = 3
EPS = 1e-05
MESH = pl.DeviceIdType.MESH
F32 = jnp.float32
BF16 = jnp.bfloat16


def peer_order(count):
    return sorted(range(1, count), key=lambda step: (abs(2 * step - count), step))


def split3(value):
    first = value.astype(BF16)
    rest = value - first.astype(F32)
    second = rest.astype(BF16)
    third = (rest - second.astype(F32)).astype(BF16)
    return first, second, third


def kernel(
    n_samp, n_bin, x_ref, gc_ref, map_ref, taps_ref, load_ref, z_ref, scores_ref,
    land, xbuf, toeplitz, band, wpad, mrows, mean, part, parts, total, totals,
    lpad, lall, lstack, cent, resid, zbuf,
    local_sem, x_sem, out_sem, send_sem, recv_sem, lsend, lrecv, psend, precv, tsend, trecv,
):
    rows, width = x_ref.shape
    share = rows // n_bin
    bins = width * n_bin
    chunks = share // CHUNK
    blocks = bins // OUT
    comps = load_ref.shape[0]
    kpad = lpad.shape[0]
    samp, me = lax.axis_index("samp"), lax.axis_index("bin")
    order = peer_order(n_bin)
    pieces = x_sem.shape[0]
    piece = rows // pieces

    def columns(index):
        return pl.ds(pl.multiple_of(index * width, width), width)

    def landed(index):
        return pl.ds(pl.multiple_of(EDGE + index * width, EDGE), width)

    own = pltpu.make_async_copy(
        x_ref.at[pl.ds(pl.multiple_of(me * share, share), share), :],
        land.at[:, landed(me)], local_sem,
    )
    loads = [
        pltpu.make_async_copy(
            x_ref.at[pl.ds(p * piece, piece), :], xbuf.at[pl.ds(p * piece, piece), :], x_sem.at[p]
        )
        for p in range(pieces)
    ]
    for copy in loads:
        copy.start()
    own.start()

    barrier = pltpu.get_barrier_semaphore()
    for step in range(1, n_bin):
        pl.semaphore_signal(
            barrier, inc=1, device_id={"bin": lax.rem(me + step, n_bin)}, device_id_type=MESH
        )
    for step in range(1, n_samp):
        pl.semaphore_signal(
            barrier, inc=1, device_id={"samp": lax.rem(samp + step, n_samp)}, device_id_type=MESH
        )
    lpad[...] = jnp.zeros(lpad.shape, BF16)
    lpad[pl.ds(0, comps), :] = load_ref[...]
    pl.semaphore_wait(barrier, n_bin + n_samp - 2)

    def load_copy(step, owner):
        return pltpu.make_async_remote_copy(
            src_ref=lpad, dst_ref=lall.at[:, columns(owner)],
            send_sem=lsend.at[step - 1], recv_sem=lrecv.at[step - 1],
            device_id={"bin": lax.rem(me + step, n_bin)}, device_id_type=MESH,
        )

    def block_copy(chunk, step, owner):
        to = lax.rem(me + step, n_bin)
        start = pl.multiple_of(to * share + chunk * CHUNK, CHUNK)
        return pltpu.make_async_remote_copy(
            src_ref=x_ref.at[pl.ds(start, CHUNK), :],
            dst_ref=land.at[pl.ds(pl.multiple_of(chunk * CHUNK, CHUNK), CHUNK), landed(owner)],
            send_sem=send_sem.at[chunk, step - 1], recv_sem=recv_sem.at[chunk, step - 1],
            device_id={"bin": to}, device_id_type=MESH,
        )

    def part_copy(step, owner):
        return pltpu.make_async_remote_copy(
            src_ref=part, dst_ref=parts.at[owner],
            send_sem=psend.at[step - 1], recv_sem=precv.at[step - 1],
            device_id={"samp": lax.rem(samp + step, n_samp)}, device_id_type=MESH,
        )

    def total_copy(step, owner):
        return pltpu.make_async_remote_copy(
            src_ref=total, dst_ref=totals.at[:, columns(owner)],
            send_sem=tsend.at[step - 1], recv_sem=trecv.at[step - 1],
            device_id={"bin": lax.rem(me + step, n_bin)}, device_id_type=MESH,
        )

    def bin_source(step):
        return lax.rem(me + n_bin - step, n_bin)

    def send_chunk(chunk):
        for step in order:
            block_copy(chunk, step, me).start()

    for step in order:
        load_copy(step, me).start()
    first = min(2, chunks)
    for chunk in range(first):
        send_chunk(chunk)

    part[...] = jnp.zeros(part.shape, F32)
    group = 128
    for p in range(pieces):
        loads[p].wait()

        def add_rows(i, carry, p=p):
            start = pl.multiple_of(p * piece + i * group, group)
            block = xbuf[pl.ds(start, group), :].astype(F32)
            part[...] += jnp.sum(block.reshape(group // 8, 8, width), axis=0)
            return carry

        lax.fori_loop(0, piece // group, add_rows, 0)
    for step in range(1, n_samp):
        part_copy(step, samp).start()
    parts[samp] = part[...]

    wpad[...] = jnp.zeros(wpad.shape, F32)
    wpad[pl.ds(0, 1), pl.ds(EDGE, bins)] = gc_ref[...] * map_ref[...]
    toeplitz[...] = jnp.zeros(toeplitz.shape, F32)
    offset = (
        lax.broadcasted_iota(jnp.int32, (WIN, OUT), 0)
        - lax.broadcasted_iota(jnp.int32, (WIN, OUT), 1)
        - (EDGE - RADIUS)
    )

    def add_tap(tap, carry):
        toeplitz[...] = jnp.where(offset == tap, taps_ref[tap], toeplitz[...])
        return carry

    lax.fori_loop(0, 2 * RADIUS + 1, add_tap, 0)

    def make_band(j, carry):
        weight = wpad[pl.ds(0, 1), pl.ds(pl.multiple_of(j * OUT, OUT), WIN)]
        tall = jnp.transpose(jnp.broadcast_to(weight, (128, WIN)))
        raw = jnp.concatenate([tall] * (OUT // 128), axis=1) * toeplitz[...]
        scaled = raw * (1.0 / jnp.sum(raw, axis=0, keepdims=True))
        upper = scaled.astype(BF16)
        band[j, pl.ds(0, WIN), :] = upper
        band[j, pl.ds(WIN, WIN), :] = (scaled - upper.astype(F32)).astype(BF16)
        return carry

    for step in range(1, n_samp):
        copy = part_copy(step, lax.rem(samp + n_samp - step, n_samp))
        copy.wait_recv()
    summed = parts[0]
    for s in range(1, n_samp):
        summed = summed + parts[s]
    total[...] = jnp.broadcast_to(jnp.sum(summed, axis=0, keepdims=True), total.shape)
    for step in order:
        total_copy(step, me).start()
    totals[:, columns(me)] = total[...]
    for chunk in range(first, min(AHEAD, chunks)):
        send_chunk(chunk)

    lax.fori_loop(0, blocks, make_band, 0)

    land[:, pl.ds(0, EDGE)] = jnp.zeros((share, EDGE), BF16)
    land[:, pl.ds(EDGE + bins, EDGE)] = jnp.zeros((share, EDGE), BF16)
    mrows[...] = jnp.zeros(mrows.shape, BF16)

    for step in order:
        load_copy(step, bin_source(step)).wait_recv()
    lall[:, columns(me)] = lpad[...]
    for copy in range(3):
        lstack[pl.ds(copy * kpad, kpad), :] = lall[...]

    for step in order:
        total_copy(step, bin_source(step)).wait_recv()
    mean_raw = totals[pl.ds(0, 1), :] / (rows * n_samp)
    for row, value in enumerate(split3(mean_raw)):
        mrows[pl.ds(row, 1), pl.ds(EDGE, bins)] = value

    def smooth(lhs, j):
        return jnp.dot(
            jnp.concatenate([lhs, lhs], axis=1), band[j], preferred_element_type=F32
        )

    def mean_block(j, carry):
        start = pl.multiple_of(j * OUT, OUT)
        value = smooth(mrows[:, pl.ds(start, WIN)], j)
        mean[:, pl.ds(start, OUT)] = jnp.broadcast_to(
            jnp.sum(value, axis=0, keepdims=True), (8, OUT)
        )
        return carry

    lax.fori_loop(0, blocks, mean_block, 0)
    own.wait()

    def lanes(value):
        folded = value[:, 0:128]
        for k in range(1, OUT // 128):
            folded = folded + value[:, k * 128:(k + 1) * 128]
        return folded

    def out_copy(chunk, slot):
        return pltpu.make_async_copy(
            zbuf.at[slot], z_ref.at[pl.ds(pl.multiple_of(chunk * CHUNK, CHUNK), CHUNK), :],
            out_sem.at[slot],
        )

    def finish(chunk, carry):
        base = pl.multiple_of(chunk * CHUNK, CHUNK)
        slot = lax.rem(chunk, 2)
        for step in order:
            block_copy(chunk, step, bin_source(step)).wait_recv()

        @pl.when(chunk + AHEAD < chunks)
        def _():
            send_chunk(chunk + AHEAD)

        def smooth_block(j, carry):
            start = pl.multiple_of(j * OUT, OUT)
            value = smooth(land[pl.ds(base, CHUNK), pl.ds(start, WIN)], j)
            cent[:, pl.ds(start, OUT)] = (
                value - mean[pl.ds(0, 1), pl.ds(start, OUT)]
            ).astype(BF16)
            return carry

        lax.fori_loop(0, blocks, smooth_block, 0, unroll=2)
        score = lax.dot_general(
            cent[...], lall[...], (((1,), (1,)), ((), ())), preferred_element_type=F32
        )
        scores_ref[pl.ds(base, CHUNK), :] = score[:, 0:comps]
        pieces3 = jnp.concatenate(split3(score), axis=1)

        def residual_block(j, acc):
            cols = pl.ds(pl.multiple_of(j * OUT, OUT), OUT)
            value = cent[:, cols].astype(F32) - jnp.dot(
                pieces3, lstack[:, cols], preferred_element_type=F32
            )
            resid[:, cols] = value
            return acc + lanes(value)

        zero = jnp.zeros((CHUNK, 128), F32)
        acc = lax.fori_loop(0, blocks, residual_block, zero, unroll=2)
        row_mean = jnp.sum(acc, axis=1, keepdims=True) / bins

        def square_block(j, acc):
            cols = pl.ds(pl.multiple_of(j * OUT, OUT), OUT)
            shifted = resid[:, cols] - row_mean
            return acc + lanes(shifted * shifted)

        acc = lax.fori_loop(0, blocks, square_block, zero, unroll=2)
        scale = 1.0 / jnp.sqrt(jnp.sum(acc, axis=1, keepdims=True) / bins + EPS)

        @pl.when(chunk >= 2)
        def _():
            out_copy(chunk - 2, slot).wait()

        def store_block(j, carry):
            cols = pl.ds(pl.multiple_of(j * OUT, OUT), OUT)
            zbuf[slot, :, cols] = ((resid[:, cols] - row_mean) * scale).astype(BF16)
            return carry

        lax.fori_loop(0, blocks, store_block, 0, unroll=2)
        out_copy(chunk, slot).start()
        return carry

    lax.fori_loop(0, chunks, finish, 0)

    def drain(chunk, carry):
        for step in order:
            block_copy(chunk, step, me).wait_send()
        return carry

    lax.fori_loop(0, chunks, drain, 0)
    for step in order:
        load_copy(step, me).wait_send()
        total_copy(step, me).wait_send()
    for step in range(1, n_samp):
        part_copy(step, samp).wait_send()
    for chunk in range(max(0, chunks - 2), chunks):
        out_copy(chunk, chunk % 2).wait()


def on_device(n_samp, n_bin, read_depth, gc_weight, map_weight, taps, loadings):
    rows, width = read_depth.shape
    comps = loadings.shape[0]
    share, bins = rows // n_bin, width * n_bin
    chunks, blocks = share // CHUNK, bins // OUT
    kpad = -(-comps // 32) * 32
    padded = bins + 2 * EDGE
    dma = pltpu.SemaphoreType.DMA
    vmem = pl.BlockSpec(memory_space=pltpu.VMEM)
    anywhere = pl.BlockSpec(memory_space=pl.ANY)
    return pl.pallas_call(
        functools.partial(kernel, n_samp, n_bin),
        out_shape=(
            jax.ShapeDtypeStruct((share, bins), BF16),
            jax.ShapeDtypeStruct((share, comps), F32),
        ),
        in_specs=[anywhere, vmem, vmem, pl.BlockSpec(memory_space=pltpu.SMEM), vmem],
        out_specs=(anywhere, vmem),
        scratch_shapes=[
            pltpu.VMEM((share, padded), BF16),
            pltpu.VMEM((rows, width), BF16),
            pltpu.VMEM((WIN, OUT), F32),
            pltpu.VMEM((blocks, 2 * WIN, OUT), BF16),
            pltpu.VMEM((8, padded), F32),
            pltpu.VMEM((16, padded), BF16),
            pltpu.VMEM((8, bins), F32),
            pltpu.VMEM((8, width), F32),
            pltpu.VMEM((n_samp, 8, width), F32),
            pltpu.VMEM((8, width), F32),
            pltpu.VMEM((8, bins), F32),
            pltpu.VMEM((kpad, width), BF16),
            pltpu.VMEM((kpad, bins), BF16),
            pltpu.VMEM((3 * kpad, bins), BF16),
            pltpu.VMEM((CHUNK, bins), BF16),
            pltpu.VMEM((CHUNK, bins), F32),
            pltpu.VMEM((2, CHUNK, bins), BF16),
            dma,
            dma((4,)),
            dma((2,)),
            dma((chunks, n_bin - 1)),
            dma((chunks, n_bin - 1)),
            dma((n_bin - 1,)),
            dma((n_bin - 1,)),
            dma((n_samp - 1,)),
            dma((n_samp - 1,)),
            dma((n_bin - 1,)),
            dma((n_bin - 1,)),
        ],
        compiler_params=pltpu.CompilerParams(
            collective_id=0, has_side_effects=True, vmem_limit_bytes=56 * 1024 * 1024
        ),
        name="denoise",
    )(
        read_depth, gc_weight.reshape(1, bins), map_weight.reshape(1, bins), taps, loadings
    )


def solution(mesh):
    return jax.shard_map(
        functools.partial(on_device, mesh.shape["samp"], mesh.shape["bin"]),
        mesh=mesh,
        in_specs=(P("samp", "bin"), P(), P(), P(), P(None, "bin")),
        out_specs=(P(("samp", "bin"), None), P(("samp", "bin"), None)),
        check_vma=False,
    )
```

```python
import functools

import jax
import jax.numpy as jnp
from jax import lax
from jax.experimental import pallas as pl
from jax.experimental.pallas import tpu as pltpu
from jax.sharding import PartitionSpec as P

RADIUS = 16
EDGE = 128
OUT = 256
WIN = OUT + 2 * EDGE
CHUNK = 128
AHEAD = 3
EPS = 1e-05
MESH = pl.DeviceIdType.MESH
F32 = jnp.float32
BF16 = jnp.bfloat16


def peer_order(count):
    return sorted(range(1, count), key=lambda step: (abs(2 * step - count), step))


def split3(value):
    first = value.astype(BF16)
    rest = value - first.astype(F32)
    second = rest.astype(BF16)
    third = (rest - second.astype(F32)).astype(BF16)
    return first, second, third


def kernel(
    n_samp, n_bin, x_ref, gc_ref, map_ref, taps_ref, load_ref, z_ref, scores_ref,
    land, xbuf, toeplitz, band, wpad, mrows, mean, part, parts, total, totals,
    lpad, lparts, lall, lstack, cent, resid, zbuf,
    local_sem, x_sem, out_sem, send_sem, recv_sem, lsend, lrecv, ssend, srecv, psend, precv, tsend, trecv,
):
    rows, width = x_ref.shape
    share = rows // n_bin
    bins = width * n_bin
    chunks = share // CHUNK
    blocks = bins // OUT
    comps = load_ref.shape[0]
    kpad = lpad.shape[0]
    lgroups = lparts.shape[0]
    lwidth = width // lgroups
    samp, me = lax.axis_index("samp"), lax.axis_index("bin")
    order = peer_order(n_bin)
    pieces = x_sem.shape[0]
    piece = rows // pieces

    def columns(index):
        return pl.ds(pl.multiple_of(index * width, width), width)

    def landed(index):
        return pl.ds(pl.multiple_of(EDGE + index * width, EDGE), width)

    own = pltpu.make_async_copy(
        x_ref.at[pl.ds(pl.multiple_of(me * share, share), share), :],
        land.at[:, landed(me)], local_sem,
    )
    slots = xbuf.shape[0]
    loads = [
        pltpu.make_async_copy(
            x_ref.at[pl.ds(p * piece, piece), :], xbuf.at[p % slots], x_sem.at[p]
        )
        for p in range(pieces)
    ]
    for copy in loads[:slots]:
        copy.start()
    own.start()

    barrier = pltpu.get_barrier_semaphore()
    for step in range(1, n_bin):
        pl.semaphore_signal(
            barrier, inc=1, device_id={"bin": lax.rem(me + step, n_bin)}, device_id_type=MESH
        )
    for step in range(1, n_samp):
        pl.semaphore_signal(
            barrier, inc=1, device_id={"samp": lax.rem(samp + step, n_samp)}, device_id_type=MESH
        )
    lpad[...] = jnp.zeros(lpad.shape, BF16)
    lpad[pl.ds(0, comps), :] = load_ref[...]

    @pl.when(samp < lgroups)
    def _():
        lparts[samp, :, pl.ds(pl.multiple_of(me * lwidth, lwidth), lwidth)] = lpad[
            :, pl.ds(pl.multiple_of(samp * lwidth, lwidth), lwidth)
        ]

    pl.semaphore_wait(barrier, n_bin + n_samp - 2)

    def load_copy(step, owner):
        return pltpu.make_async_remote_copy(
            src_ref=lpad.at[:, pl.ds(pl.multiple_of(samp * lwidth, lwidth), lwidth)],
            dst_ref=lparts.at[samp, :, pl.ds(pl.multiple_of(owner * lwidth, lwidth), lwidth)],
            send_sem=lsend.at[step - 1], recv_sem=lrecv.at[step - 1],
            device_id={"bin": lax.rem(me + step, n_bin)}, device_id_type=MESH,
        )

    def spread_copy(step, owner):
        return pltpu.make_async_remote_copy(
            src_ref=lparts.at[owner], dst_ref=lparts.at[owner],
            send_sem=ssend.at[step - 1], recv_sem=srecv.at[step - 1],
            device_id={"samp": lax.rem(samp + step, n_samp)}, device_id_type=MESH,
        )

    def block_copy(chunk, step, owner):
        to = lax.rem(me + step, n_bin)
        start = pl.multiple_of(to * share + chunk * CHUNK, CHUNK)
        return pltpu.make_async_remote_copy(
            src_ref=x_ref.at[pl.ds(start, CHUNK), :],
            dst_ref=land.at[pl.ds(pl.multiple_of(chunk * CHUNK, CHUNK), CHUNK), landed(owner)],
            send_sem=send_sem.at[chunk, step - 1], recv_sem=recv_sem.at[chunk, step - 1],
            device_id={"bin": to}, device_id_type=MESH,
        )

    def part_copy(step, owner):
        return pltpu.make_async_remote_copy(
            src_ref=part, dst_ref=parts.at[owner],
            send_sem=psend.at[step - 1], recv_sem=precv.at[step - 1],
            device_id={"samp": lax.rem(samp + step, n_samp)}, device_id_type=MESH,
        )

    def total_copy(step, owner):
        return pltpu.make_async_remote_copy(
            src_ref=total, dst_ref=totals.at[:, columns(owner)],
            send_sem=tsend.at[step - 1], recv_sem=trecv.at[step - 1],
            device_id={"bin": lax.rem(me + step, n_bin)}, device_id_type=MESH,
        )

    def bin_source(step):
        return lax.rem(me + n_bin - step, n_bin)

    def send_chunk(chunk):
        for step in order:
            block_copy(chunk, step, me).start()

    @pl.when(samp < lgroups)
    def _():
        for step in order:
            load_copy(step, me).start()

    first = min(2, chunks)
    for chunk in range(first):
        send_chunk(chunk)

    part[...] = jnp.zeros(part.shape, F32)
    group = 128
    for p in range(pieces):
        loads[p].wait()

        def add_rows(i, carry, p=p):
            start = pl.multiple_of(i * group, group)
            block = xbuf[p % slots, pl.ds(start, group), :].astype(F32)
            part[...] += jnp.sum(block.reshape(group // 8, 8, width), axis=0)
            return carry

        lax.fori_loop(0, piece // group, add_rows, 0)
        if p + slots < pieces:
            loads[p + slots].start()
    for step in range(1, n_samp):
        part_copy(step, samp).start()
    parts[samp] = part[...]

    wpad[...] = jnp.zeros(wpad.shape, F32)
    wpad[pl.ds(0, 1), pl.ds(EDGE, bins)] = gc_ref[...] * map_ref[...]
    toeplitz[...] = jnp.zeros(toeplitz.shape, F32)
    offset = (
        lax.broadcasted_iota(jnp.int32, (WIN, OUT), 0)
        - lax.broadcasted_iota(jnp.int32, (WIN, OUT), 1)
        - (EDGE - RADIUS)
    )

    def add_tap(tap, carry):
        toeplitz[...] = jnp.where(offset == tap, taps_ref[tap], toeplitz[...])
        return carry

    lax.fori_loop(0, 2 * RADIUS + 1, add_tap, 0)

    def make_band(j, carry):
        weight = wpad[pl.ds(0, 1), pl.ds(pl.multiple_of(j * OUT, OUT), WIN)]
        tall = jnp.transpose(jnp.broadcast_to(weight, (128, WIN)))
        raw = jnp.concatenate([tall] * (OUT // 128), axis=1) * toeplitz[...]
        scaled = raw * (1.0 / jnp.sum(raw, axis=0, keepdims=True))
        upper = scaled.astype(BF16)
        band[j, pl.ds(0, WIN), :] = upper
        band[j, pl.ds(WIN, WIN), :] = (scaled - upper.astype(F32)).astype(BF16)
        return carry

    for step in range(1, n_samp):
        copy = part_copy(step, lax.rem(samp + n_samp - step, n_samp))
        copy.wait_recv()
    summed = parts[0]
    for s in range(1, n_samp):
        summed = summed + parts[s]
    total[...] = jnp.sum(summed, axis=0, keepdims=True)
    for step in order:
        total_copy(step, me).start()
    totals[:, columns(me)] = total[...]
    for chunk in range(first, min(AHEAD, chunks)):
        send_chunk(chunk)

    @pl.when(samp < lgroups)
    def _():
        for step in order:
            load_copy(step, bin_source(step)).wait_recv()
        for step in range(1, n_samp):
            spread_copy(step, samp).start()

    lax.fori_loop(0, blocks, make_band, 0)

    land[:, pl.ds(0, EDGE)] = jnp.zeros((share, EDGE), BF16)
    land[:, pl.ds(EDGE + bins, EDGE)] = jnp.zeros((share, EDGE), BF16)
    mrows[...] = jnp.zeros(mrows.shape, BF16)

    for step in range(1, n_samp):
        owner = lax.rem(samp + n_samp - step, n_samp)

        @pl.when(owner < lgroups)
        def _(step=step, owner=owner):
            spread_copy(step, owner).wait_recv()

    for b in range(n_bin):
        for g in range(lgroups):
            lall[:, pl.ds(b * width + g * lwidth, lwidth)] = lparts[
                g, :, pl.ds(b * lwidth, lwidth)
            ]
    for copy in range(3):
        lstack[pl.ds(copy * kpad, kpad), :] = lall[...]

    for step in order:
        total_copy(step, bin_source(step)).wait_recv()
    mean_raw = totals[...] / (rows * n_samp)
    for row, value in enumerate(split3(mean_raw)):
        mrows[pl.ds(row, 1), pl.ds(EDGE, bins)] = value

    def smooth(lhs, j):
        return jnp.dot(
            jnp.concatenate([lhs, lhs], axis=1), band[j], preferred_element_type=F32
        )

    def mean_block(j, carry):
        start = pl.multiple_of(j * OUT, OUT)
        value = smooth(mrows[:, pl.ds(start, WIN)], j)
        mean[:, pl.ds(start, OUT)] = jnp.broadcast_to(
            jnp.sum(value, axis=0, keepdims=True), (8, OUT)
        )
        return carry

    lax.fori_loop(0, blocks, mean_block, 0)
    own.wait()

    def lanes(value):
        folded = value[:, 0:128]
        for k in range(1, OUT // 128):
            folded = folded + value[:, k * 128:(k + 1) * 128]
        return folded

    def out_copy(chunk, slot):
        return pltpu.make_async_copy(
            zbuf.at[slot], z_ref.at[pl.ds(pl.multiple_of(chunk * CHUNK, CHUNK), CHUNK), :],
            out_sem.at[slot],
        )

    def finish(chunk, carry):
        base = pl.multiple_of(chunk * CHUNK, CHUNK)
        slot = lax.rem(chunk, 2)
        for step in order:
            block_copy(chunk, step, bin_source(step)).wait_recv()

        @pl.when(chunk + AHEAD < chunks)
        def _():
            send_chunk(chunk + AHEAD)

        def smooth_block(j, carry):
            start = pl.multiple_of(j * OUT, OUT)
            value = smooth(land[pl.ds(base, CHUNK), pl.ds(start, WIN)], j)
            cent[:, pl.ds(start, OUT)] = (
                value - mean[pl.ds(0, 1), pl.ds(start, OUT)]
            ).astype(BF16)
            return carry

        lax.fori_loop(0, blocks, smooth_block, 0, unroll=2)
        score = lax.dot_general(
            cent[...], lall[...], (((1,), (1,)), ((), ())), preferred_element_type=F32
        )
        scores_ref[:, pl.ds(base, CHUNK)] = jnp.transpose(score)[0:comps, :]
        pieces3 = jnp.concatenate(split3(score), axis=1)

        def residual_block(j, acc):
            cols = pl.ds(pl.multiple_of(j * OUT, OUT), OUT)
            value = cent[:, cols].astype(F32) - jnp.dot(
                pieces3, lstack[:, cols], preferred_element_type=F32
            )
            resid[:, cols] = value
            return acc + lanes(value)

        zero = jnp.zeros((CHUNK, 128), F32)
        acc = lax.fori_loop(0, blocks, residual_block, zero, unroll=2)
        row_mean = jnp.sum(acc, axis=1, keepdims=True) / bins

        def square_block(j, acc):
            cols = pl.ds(pl.multiple_of(j * OUT, OUT), OUT)
            shifted = resid[:, cols] - row_mean
            return acc + lanes(shifted * shifted)

        acc = lax.fori_loop(0, blocks, square_block, zero, unroll=2)
        scale = 1.0 / jnp.sqrt(jnp.sum(acc, axis=1, keepdims=True) / bins + EPS)

        @pl.when(chunk >= 2)
        def _():
            out_copy(chunk - 2, slot).wait()

        def store_block(j, carry):
            cols = pl.ds(pl.multiple_of(j * OUT, OUT), OUT)
            zbuf[slot, :, cols] = ((resid[:, cols] - row_mean) * scale).astype(BF16)
            return carry

        lax.fori_loop(0, blocks, store_block, 0, unroll=2)
        out_copy(chunk, slot).start()
        return carry

    lax.fori_loop(0, chunks, finish, 0)

    def drain(chunk, carry):
        for step in order:
            block_copy(chunk, step, me).wait_send()
        return carry

    lax.fori_loop(0, chunks, drain, 0)
    for step in order:
        total_copy(step, me).wait_send()

    @pl.when(samp < lgroups)
    def _():
        for step in order:
            load_copy(step, me).wait_send()
        for step in range(1, n_samp):
            spread_copy(step, samp).wait_send()

    for step in range(1, n_samp):
        part_copy(step, samp).wait_send()
    for chunk in range(max(0, chunks - 2), chunks):
        out_copy(chunk, chunk % 2).wait()


def on_device(n_samp, n_bin, read_depth, gc_weight, map_weight, taps, loadings):
    rows, width = read_depth.shape
    comps = loadings.shape[0]
    share, bins = rows // n_bin, width * n_bin
    chunks, blocks = share // CHUNK, bins // OUT
    lgroups = min(n_samp, width // 128)
    kpad = -(-comps // 32) * 32
    padded = bins + 2 * EDGE
    dma = pltpu.SemaphoreType.DMA
    vmem = pl.BlockSpec(memory_space=pltpu.VMEM)
    anywhere = pl.BlockSpec(memory_space=pl.ANY)
    zscore, scores = pl.pallas_call(
        functools.partial(kernel, n_samp, n_bin),
        out_shape=(
            jax.ShapeDtypeStruct((share, bins), BF16),
            jax.ShapeDtypeStruct((comps, share), F32),
        ),
        in_specs=[anywhere, vmem, vmem, pl.BlockSpec(memory_space=pltpu.SMEM), vmem],
        out_specs=(anywhere, vmem),
        scratch_shapes=[
            pltpu.VMEM((share, padded), BF16),
            pltpu.VMEM((2, rows // 8, width), BF16),
            pltpu.VMEM((WIN, OUT), F32),
            pltpu.VMEM((blocks, 2 * WIN, OUT), BF16),
            pltpu.VMEM((8, padded), F32),
            pltpu.VMEM((16, padded), BF16),
            pltpu.VMEM((8, bins), F32),
            pltpu.VMEM((8, width), F32),
            pltpu.VMEM((n_samp, 8, width), F32),
            pltpu.VMEM((1, width), F32),
            pltpu.VMEM((1, bins), F32),
            pltpu.VMEM((kpad, width), BF16),
            pltpu.VMEM((lgroups, kpad, width * n_bin // lgroups), BF16),
            pltpu.VMEM((kpad, bins), BF16),
            pltpu.VMEM((3 * kpad, bins), BF16),
            pltpu.VMEM((CHUNK, bins), BF16),
            pltpu.VMEM((CHUNK, bins), F32),
            pltpu.VMEM((2, CHUNK, bins), BF16),
            dma,
            dma((8,)),
            dma((2,)),
            dma((chunks, n_bin - 1)),
            dma((chunks, n_bin - 1)),
            dma((n_bin - 1,)),
            dma((n_bin - 1,)),
            dma((n_samp - 1,)),
            dma((n_samp - 1,)),
            dma((n_samp - 1,)),
            dma((n_samp - 1,)),
            dma((n_bin - 1,)),
            dma((n_bin - 1,)),
        ],
        compiler_params=pltpu.CompilerParams(
            collective_id=0, has_side_effects=True, vmem_limit_bytes=48 * 1024 * 1024
        ),
        name="denoise",
    )(
        read_depth, gc_weight.reshape(1, bins), map_weight.reshape(1, bins), taps, loadings
    )
    return zscore, scores.T


def solution(mesh):
    return jax.shard_map(
        functools.partial(on_device, mesh.shape["samp"], mesh.shape["bin"]),
        mesh=mesh,
        in_specs=(P("samp", "bin"), P(), P(), P(), P(None, "bin")),
        out_specs=(P(("samp", "bin"), None), P(("samp", "bin"), None)),
        check_vma=False,
    )
```

```python
import functools

import jax
import jax.numpy as jnp
from jax import lax
from jax.experimental import pallas as pl
from jax.experimental.pallas import tpu as pltpu
from jax.sharding import PartitionSpec as P

RADIUS = 16
EDGE = 128
OUT = 256
WIN = OUT + 2 * EDGE
CHUNK = 128
AHEAD = 3
EPS = 1e-05
MESH = pl.DeviceIdType.MESH
F32 = jnp.float32
BF16 = jnp.bfloat16


def peer_order(count):
    return sorted(range(1, count), key=lambda step: (abs(2 * step - count), step))


def split3(value):
    first = value.astype(BF16)
    rest = value - first.astype(F32)
    second = rest.astype(BF16)
    third = (rest - second.astype(F32)).astype(BF16)
    return first, second, third


def kernel(
    n_samp, n_bin, x_ref, gc_ref, map_ref, taps_ref, load_ref, z_ref, scores_ref,
    land, xbuf, toeplitz, band, wpad, mrows, mean, part, parts, total, totals,
    lpad, lparts, lall, lstack, cent, resid,
    local_sem, x_sem, send_sem, recv_sem, lsend, lrecv, ssend, srecv, psend, precv, tsend, trecv,
):
    rows, width = x_ref.shape
    share = rows // n_bin
    bins = width * n_bin
    chunks = share // CHUNK
    blocks = bins // OUT
    comps = load_ref.shape[0]
    kpad = lpad.shape[0]
    lgroups = lparts.shape[0]
    lwidth = width // lgroups
    samp, me = lax.axis_index("samp"), lax.axis_index("bin")
    order = peer_order(n_bin)
    pieces = x_sem.shape[0]
    piece = rows // pieces

    def columns(index):
        return pl.ds(pl.multiple_of(index * width, width), width)

    def landed(index):
        return pl.ds(pl.multiple_of(EDGE + index * width, EDGE), width)

    own = pltpu.make_async_copy(
        x_ref.at[pl.ds(pl.multiple_of(me * share, share), share), :],
        land.at[:, landed(me)], local_sem,
    )
    slots = xbuf.shape[0]
    loads = [
        pltpu.make_async_copy(
            x_ref.at[pl.ds(p * piece, piece), :], xbuf.at[p % slots], x_sem.at[p]
        )
        for p in range(pieces)
    ]
    for copy in loads[:slots]:
        copy.start()
    own.start()

    barrier = pltpu.get_barrier_semaphore()
    for step in range(1, n_bin):
        pl.semaphore_signal(
            barrier, inc=1, device_id={"bin": lax.rem(me + step, n_bin)}, device_id_type=MESH
        )
    for step in range(1, n_samp):
        pl.semaphore_signal(
            barrier, inc=1, device_id={"samp": lax.rem(samp + step, n_samp)}, device_id_type=MESH
        )
    lpad[...] = jnp.zeros(lpad.shape, BF16)
    lpad[pl.ds(0, comps), :] = load_ref[...]

    @pl.when(samp < lgroups)
    def _():
        lparts[samp, :, pl.ds(pl.multiple_of(me * lwidth, lwidth), lwidth)] = lpad[
            :, pl.ds(pl.multiple_of(samp * lwidth, lwidth), lwidth)
        ]

    pl.semaphore_wait(barrier, n_bin + n_samp - 2)

    def load_copy(step, owner):
        return pltpu.make_async_remote_copy(
            src_ref=lpad.at[:, pl.ds(pl.multiple_of(samp * lwidth, lwidth), lwidth)],
            dst_ref=lparts.at[samp, :, pl.ds(pl.multiple_of(owner * lwidth, lwidth), lwidth)],
            send_sem=lsend.at[step - 1], recv_sem=lrecv.at[step - 1],
            device_id={"bin": lax.rem(me + step, n_bin)}, device_id_type=MESH,
        )

    def spread_copy(step, owner):
        return pltpu.make_async_remote_copy(
            src_ref=lparts.at[owner], dst_ref=lparts.at[owner],
            send_sem=ssend.at[step - 1], recv_sem=srecv.at[step - 1],
            device_id={"samp": lax.rem(samp + step, n_samp)}, device_id_type=MESH,
        )

    def block_copy(chunk, step, owner):
        to = lax.rem(me + step, n_bin)
        start = pl.multiple_of(to * share + chunk * CHUNK, CHUNK)
        return pltpu.make_async_remote_copy(
            src_ref=x_ref.at[pl.ds(start, CHUNK), :],
            dst_ref=land.at[pl.ds(pl.multiple_of(chunk * CHUNK, CHUNK), CHUNK), landed(owner)],
            send_sem=send_sem.at[chunk, step - 1], recv_sem=recv_sem.at[chunk, step - 1],
            device_id={"bin": to}, device_id_type=MESH,
        )

    def part_copy(step, owner):
        return pltpu.make_async_remote_copy(
            src_ref=part, dst_ref=parts.at[owner],
            send_sem=psend.at[step - 1], recv_sem=precv.at[step - 1],
            device_id={"samp": lax.rem(samp + step, n_samp)}, device_id_type=MESH,
        )

    def total_copy(step, owner):
        return pltpu.make_async_remote_copy(
            src_ref=total, dst_ref=totals.at[:, columns(owner)],
            send_sem=tsend.at[step - 1], recv_sem=trecv.at[step - 1],
            device_id={"bin": lax.rem(me + step, n_bin)}, device_id_type=MESH,
        )

    def bin_source(step):
        return lax.rem(me + n_bin - step, n_bin)

    def send_chunk(chunk):
        for step in order:
            block_copy(chunk, step, me).start()

    @pl.when(samp < lgroups)
    def _():
        for step in order:
            load_copy(step, me).start()

    first = min(2, chunks)
    for chunk in range(first):
        send_chunk(chunk)

    part[...] = jnp.zeros(part.shape, F32)
    group = 128
    for p in range(pieces):
        loads[p].wait()

        def add_rows(i, carry, p=p):
            start = pl.multiple_of(i * group, group)
            block = xbuf[p % slots, pl.ds(start, group), :].astype(F32)
            part[...] += jnp.sum(block.reshape(group // 8, 8, width), axis=0)
            return carry

        lax.fori_loop(0, piece // group, add_rows, 0)
        if p + slots < pieces:
            loads[p + slots].start()
    for step in range(1, n_samp):
        part_copy(step, samp).start()
    parts[samp] = part[...]

    wpad[...] = jnp.zeros(wpad.shape, F32)
    wpad[pl.ds(0, 1), pl.ds(EDGE, bins)] = gc_ref[...] * map_ref[...]
    toeplitz[...] = jnp.zeros(toeplitz.shape, F32)
    offset = (
        lax.broadcasted_iota(jnp.int32, (WIN, OUT), 0)
        - lax.broadcasted_iota(jnp.int32, (WIN, OUT), 1)
        - (EDGE - RADIUS)
    )

    def add_tap(tap, carry):
        toeplitz[...] = jnp.where(offset == tap, taps_ref[tap], toeplitz[...])
        return carry

    lax.fori_loop(0, 2 * RADIUS + 1, add_tap, 0)

    def make_band(j, carry):
        weight = wpad[pl.ds(0, 1), pl.ds(pl.multiple_of(j * OUT, OUT), WIN)]
        tall = jnp.transpose(jnp.broadcast_to(weight, (128, WIN)))
        raw = jnp.concatenate([tall] * (OUT // 128), axis=1) * toeplitz[...]
        scaled = raw * (1.0 / jnp.sum(raw, axis=0, keepdims=True))
        upper = scaled.astype(BF16)
        band[j, pl.ds(0, WIN), :] = upper
        band[j, pl.ds(WIN, WIN), :] = (scaled - upper.astype(F32)).astype(BF16)
        return carry

    for step in range(1, n_samp):
        copy = part_copy(step, lax.rem(samp + n_samp - step, n_samp))
        copy.wait_recv()
    summed = parts[0]
    for s in range(1, n_samp):
        summed = summed + parts[s]
    total[...] = jnp.sum(summed, axis=0, keepdims=True)
    for step in order:
        total_copy(step, me).start()
    totals[:, columns(me)] = total[...]
    for chunk in range(first, min(AHEAD, chunks)):
        send_chunk(chunk)

    @pl.when(samp < lgroups)
    def _():
        for step in order:
            load_copy(step, bin_source(step)).wait_recv()
        for step in range(1, n_samp):
            spread_copy(step, samp).start()

    lax.fori_loop(0, blocks, make_band, 0)

    land[:, pl.ds(0, EDGE)] = jnp.zeros((share, EDGE), BF16)
    land[:, pl.ds(EDGE + bins, EDGE)] = jnp.zeros((share, EDGE), BF16)
    mrows[...] = jnp.zeros(mrows.shape, BF16)

    for step in range(1, n_samp):
        owner = lax.rem(samp + n_samp - step, n_samp)

        @pl.when(owner < lgroups)
        def _(step=step, owner=owner):
            spread_copy(step, owner).wait_recv()

    for b in range(n_bin):
        for g in range(lgroups):
            lall[:, pl.ds(b * width + g * lwidth, lwidth)] = lparts[
                g, :, pl.ds(b * lwidth, lwidth)
            ]
    for copy in range(3):
        lstack[pl.ds(copy * kpad, kpad), :] = lall[...]

    for step in order:
        total_copy(step, bin_source(step)).wait_recv()
    mean_raw = totals[...] / (rows * n_samp)
    for row, value in enumerate(split3(mean_raw)):
        mrows[pl.ds(row, 1), pl.ds(EDGE, bins)] = value

    def smooth(lhs, j):
        return jnp.dot(
            jnp.concatenate([lhs, lhs], axis=1), band[j], preferred_element_type=F32
        )

    def mean_block(j, carry):
        start = pl.multiple_of(j * OUT, OUT)
        value = smooth(mrows[:, pl.ds(start, WIN)], j)
        mean[:, pl.ds(start, OUT)] = jnp.broadcast_to(
            jnp.sum(value, axis=0, keepdims=True), (8, OUT)
        )
        return carry

    lax.fori_loop(0, blocks, mean_block, 0)
    own.wait()

    def lanes(value):
        folded = value[:, 0:128]
        for k in range(1, OUT // 128):
            folded = folded + value[:, k * 128:(k + 1) * 128]
        return folded

    def finish(chunk, carry):
        base = pl.multiple_of(chunk * CHUNK, CHUNK)
        for step in order:
            block_copy(chunk, step, bin_source(step)).wait_recv()

        @pl.when(chunk + AHEAD < chunks)
        def _():
            send_chunk(chunk + AHEAD)

        def smooth_block(j, carry):
            start = pl.multiple_of(j * OUT, OUT)
            value = smooth(land[pl.ds(base, CHUNK), pl.ds(start, WIN)], j)
            cent[:, pl.ds(start, OUT)] = (
                value - mean[pl.ds(0, 1), pl.ds(start, OUT)]
            ).astype(BF16)
            return carry

        lax.fori_loop(0, blocks, smooth_block, 0, unroll=2)
        score = lax.dot_general(
            cent[...], lall[...], (((1,), (1,)), ((), ())), preferred_element_type=F32
        )
        scores_ref[:, pl.ds(base, CHUNK)] = jnp.transpose(score)[0:comps, :]
        pieces3 = jnp.concatenate(split3(score), axis=1)

        def residual_block(j, acc):
            cols = pl.ds(pl.multiple_of(j * OUT, OUT), OUT)
            value = cent[:, cols].astype(F32) - jnp.dot(
                pieces3, lstack[:, cols], preferred_element_type=F32
            )
            resid[:, cols] = value
            return acc + lanes(value)

        zero = jnp.zeros((CHUNK, 128), F32)
        acc = lax.fori_loop(0, blocks, residual_block, zero, unroll=2)
        row_mean = jnp.sum(acc, axis=1, keepdims=True) / bins

        def square_block(j, acc):
            cols = pl.ds(pl.multiple_of(j * OUT, OUT), OUT)
            shifted = resid[:, cols] - row_mean
            return acc + lanes(shifted * shifted)

        acc = lax.fori_loop(0, blocks, square_block, zero, unroll=2)
        scale = 1.0 / jnp.sqrt(jnp.sum(acc, axis=1, keepdims=True) / bins + EPS)

        def store_block(j, carry):
            cols = pl.ds(pl.multiple_of(j * OUT, OUT), OUT)
            z_ref[pl.ds(base, CHUNK), cols] = ((resid[:, cols] - row_mean) * scale).astype(BF16)
            return carry

        lax.fori_loop(0, blocks, store_block, 0, unroll=2)
        return carry

    lax.fori_loop(0, chunks, finish, 0)

    def drain(chunk, carry):
        for step in order:
            block_copy(chunk, step, me).wait_send()
        return carry

    lax.fori_loop(0, chunks, drain, 0)
    for step in order:
        total_copy(step, me).wait_send()

    @pl.when(samp < lgroups)
    def _():
        for step in order:
            load_copy(step, me).wait_send()
        for step in range(1, n_samp):
            spread_copy(step, samp).wait_send()

    for step in range(1, n_samp):
        part_copy(step, samp).wait_send()


def on_device(n_samp, n_bin, read_depth, gc_weight, map_weight, taps, loadings):
    rows, width = read_depth.shape
    comps = loadings.shape[0]
    share, bins = rows // n_bin, width * n_bin
    chunks, blocks = share // CHUNK, bins // OUT
    lgroups = min(n_samp, width // 128)
    kpad = -(-comps // 32) * 32
    padded = bins + 2 * EDGE
    dma = pltpu.SemaphoreType.DMA
    vmem = pl.BlockSpec(memory_space=pltpu.VMEM)
    anywhere = pl.BlockSpec(memory_space=pl.ANY)
    zscore, scores = pl.pallas_call(
        functools.partial(kernel, n_samp, n_bin),
        out_shape=(
            pltpu.VMEM((share, bins), BF16),
            pltpu.VMEM((comps, share), F32),
        ),
        in_specs=[anywhere, vmem, vmem, pl.BlockSpec(memory_space=pltpu.SMEM), vmem],
        out_specs=(vmem, vmem),
        scratch_shapes=[
            pltpu.VMEM((share, padded), BF16),
            pltpu.VMEM((2, rows // 8, width), BF16),
            pltpu.VMEM((WIN, OUT), F32),
            pltpu.VMEM((blocks, 2 * WIN, OUT), BF16),
            pltpu.VMEM((8, padded), F32),
            pltpu.VMEM((16, padded), BF16),
            pltpu.VMEM((8, bins), F32),
            pltpu.VMEM((8, width), F32),
            pltpu.VMEM((n_samp, 8, width), F32),
            pltpu.VMEM((1, width), F32),
            pltpu.VMEM((1, bins), F32),
            pltpu.VMEM((kpad, width), BF16),
            pltpu.VMEM((lgroups, kpad, width * n_bin // lgroups), BF16),
            pltpu.VMEM((kpad, bins), BF16),
            pltpu.VMEM((3 * kpad, bins), BF16),
            pltpu.VMEM((CHUNK, bins), BF16),
            pltpu.VMEM((CHUNK, bins), F32),
            dma,
            dma((8,)),
            dma((chunks, n_bin - 1)),
            dma((chunks, n_bin - 1)),
            dma((n_bin - 1,)),
            dma((n_bin - 1,)),
            dma((n_samp - 1,)),
            dma((n_samp - 1,)),
            dma((n_samp - 1,)),
            dma((n_samp - 1,)),
            dma((n_bin - 1,)),
            dma((n_bin - 1,)),
        ],
        compiler_params=pltpu.CompilerParams(
            collective_id=0, has_side_effects=True, vmem_limit_bytes=48 * 1024 * 1024
        ),
        name="denoise",
    )(
        read_depth, gc_weight.reshape(1, bins), map_weight.reshape(1, bins), taps, loadings
    )
    return zscore, scores.T


def solution(mesh):
    return jax.shard_map(
        functools.partial(on_device, mesh.shape["samp"], mesh.shape["bin"]),
        mesh=mesh,
        in_specs=(P("samp", "bin"), P(), P(), P(), P(None, "bin")),
        out_specs=(P(("samp", "bin"), None), P(("samp", "bin"), None)),
        check_vma=False,
    )
```

```python
import functools

import jax
import jax.numpy as jnp
from jax import lax
from jax.experimental import pallas as pl
from jax.experimental.pallas import tpu as pltpu
from jax.sharding import PartitionSpec as P

RADIUS = 16
EDGE = 128
OUT = 256
WIN = OUT + 2 * EDGE
CHUNK = 128
AHEAD = 3
TAIL = ((0, 64), (64, 32), (96, 32))
EPS = 1e-05
MESH = pl.DeviceIdType.MESH
F32 = jnp.float32
BF16 = jnp.bfloat16


def peer_order(count):
    return sorted(range(1, count), key=lambda step: (abs(2 * step - count), step))


def split3(value):
    first = value.astype(BF16)
    rest = value - first.astype(F32)
    second = rest.astype(BF16)
    third = (rest - second.astype(F32)).astype(BF16)
    return first, second, third


def kernel(
    n_samp, n_bin, x_ref, gc_ref, map_ref, taps_ref, load_ref, z_ref, scores_ref,
    land, xbuf, toeplitz, band, wpad, mrows, mean, part, parts, total, totals,
    lpad, lparts, lall, lstack, cent, resid,
    local_sem, x_sem, send_sem, recv_sem, tail_send, tail_recv, lsend, lrecv, ssend, srecv, psend, precv, tsend, trecv,
):
    rows, width = x_ref.shape
    share = rows // n_bin
    bins = width * n_bin
    chunks = share // CHUNK
    blocks = bins // OUT
    comps = load_ref.shape[0]
    kpad = lpad.shape[0]
    lgroups = lparts.shape[0]
    lwidth = width // lgroups
    samp, me = lax.axis_index("samp"), lax.axis_index("bin")
    order = peer_order(n_bin)
    pieces = x_sem.shape[0]
    piece = rows // pieces

    def columns(index):
        return pl.ds(pl.multiple_of(index * width, width), width)

    def landed(index):
        return pl.ds(pl.multiple_of(EDGE + index * width, EDGE), width)

    own = pltpu.make_async_copy(
        x_ref.at[pl.ds(pl.multiple_of(me * share, share), share), :],
        land.at[:, landed(me)], local_sem,
    )
    slots = xbuf.shape[0]
    loads = [
        pltpu.make_async_copy(
            x_ref.at[pl.ds(p * piece, piece), :], xbuf.at[p % slots], x_sem.at[p]
        )
        for p in range(pieces)
    ]
    for copy in loads[:slots]:
        copy.start()
    own.start()

    barrier = pltpu.get_barrier_semaphore()
    for step in range(1, n_bin):
        pl.semaphore_signal(
            barrier, inc=1, device_id={"bin": lax.rem(me + step, n_bin)}, device_id_type=MESH
        )
    for step in range(1, n_samp):
        pl.semaphore_signal(
            barrier, inc=1, device_id={"samp": lax.rem(samp + step, n_samp)}, device_id_type=MESH
        )
    lpad[...] = jnp.zeros(lpad.shape, BF16)
    lpad[pl.ds(0, comps), :] = load_ref[...]

    @pl.when(samp < lgroups)
    def _():
        lparts[samp, :, pl.ds(pl.multiple_of(me * lwidth, lwidth), lwidth)] = lpad[
            :, pl.ds(pl.multiple_of(samp * lwidth, lwidth), lwidth)
        ]

    pl.semaphore_wait(barrier, n_bin + n_samp - 2)

    def load_copy(step, owner):
        return pltpu.make_async_remote_copy(
            src_ref=lpad.at[:, pl.ds(pl.multiple_of(samp * lwidth, lwidth), lwidth)],
            dst_ref=lparts.at[samp, :, pl.ds(pl.multiple_of(owner * lwidth, lwidth), lwidth)],
            send_sem=lsend.at[step - 1], recv_sem=lrecv.at[step - 1],
            device_id={"bin": lax.rem(me + step, n_bin)}, device_id_type=MESH,
        )

    def spread_copy(step, owner):
        return pltpu.make_async_remote_copy(
            src_ref=lparts.at[owner], dst_ref=lparts.at[owner],
            send_sem=ssend.at[step - 1], recv_sem=srecv.at[step - 1],
            device_id={"samp": lax.rem(samp + step, n_samp)}, device_id_type=MESH,
        )

    def block_copy(chunk, step, owner):
        to = lax.rem(me + step, n_bin)
        start = pl.multiple_of(to * share + chunk * CHUNK, CHUNK)
        return pltpu.make_async_remote_copy(
            src_ref=x_ref.at[pl.ds(start, CHUNK), :],
            dst_ref=land.at[pl.ds(pl.multiple_of(chunk * CHUNK, CHUNK), CHUNK), landed(owner)],
            send_sem=send_sem.at[chunk, step - 1], recv_sem=recv_sem.at[chunk, step - 1],
            device_id={"bin": to}, device_id_type=MESH,
        )

    def tail_copy(index, step, owner):
        to = lax.rem(me + step, n_bin)
        offset, size = TAIL[index]
        offset = offset + share - CHUNK
        start = pl.multiple_of(to * share + offset, size)
        return pltpu.make_async_remote_copy(
            src_ref=x_ref.at[pl.ds(start, size), :],
            dst_ref=land.at[pl.ds(offset, size), landed(owner)],
            send_sem=tail_send.at[index, step - 1], recv_sem=tail_recv.at[index, step - 1],
            device_id={"bin": to}, device_id_type=MESH,
        )

    def send_tail():
        for index in range(len(TAIL)):
            for step in order:
                tail_copy(index, step, me).start()

    def part_copy(step, owner):
        return pltpu.make_async_remote_copy(
            src_ref=part, dst_ref=parts.at[owner],
            send_sem=psend.at[step - 1], recv_sem=precv.at[step - 1],
            device_id={"samp": lax.rem(samp + step, n_samp)}, device_id_type=MESH,
        )

    def total_copy(step, owner):
        return pltpu.make_async_remote_copy(
            src_ref=total, dst_ref=totals.at[:, columns(owner)],
            send_sem=tsend.at[step - 1], recv_sem=trecv.at[step - 1],
            device_id={"bin": lax.rem(me + step, n_bin)}, device_id_type=MESH,
        )

    def bin_source(step):
        return lax.rem(me + n_bin - step, n_bin)

    def send_chunk(chunk):
        for step in order:
            block_copy(chunk, step, me).start()

    @pl.when(samp < lgroups)
    def _():
        for step in order:
            load_copy(step, me).start()

    first = min(2, chunks)
    for chunk in range(first):
        send_chunk(chunk)

    part[...] = jnp.zeros(part.shape, F32)
    group = 128
    for p in range(pieces):
        loads[p].wait()

        def add_rows(i, carry, p=p):
            start = pl.multiple_of(i * group, group)
            block = xbuf[p % slots, pl.ds(start, group), :].astype(F32)
            part[...] += jnp.sum(block.reshape(group // 8, 8, width), axis=0)
            return carry

        lax.fori_loop(0, piece // group, add_rows, 0)
        if p + slots < pieces:
            loads[p + slots].start()
    for step in range(1, n_samp):
        part_copy(step, samp).start()
    parts[samp] = part[...]

    wpad[...] = jnp.zeros(wpad.shape, F32)
    wpad[pl.ds(0, 1), pl.ds(EDGE, bins)] = gc_ref[...] * map_ref[...]
    toeplitz[...] = jnp.zeros(toeplitz.shape, F32)
    offset = (
        lax.broadcasted_iota(jnp.int32, (WIN, OUT), 0)
        - lax.broadcasted_iota(jnp.int32, (WIN, OUT), 1)
        - (EDGE - RADIUS)
    )

    def add_tap(tap, carry):
        toeplitz[...] = jnp.where(offset == tap, taps_ref[tap], toeplitz[...])
        return carry

    lax.fori_loop(0, 2 * RADIUS + 1, add_tap, 0)

    def make_band(j, carry):
        weight = wpad[pl.ds(0, 1), pl.ds(pl.multiple_of(j * OUT, OUT), WIN)]
        tall = jnp.transpose(jnp.broadcast_to(weight, (128, WIN)))
        raw = jnp.concatenate([tall] * (OUT // 128), axis=1) * toeplitz[...]
        scaled = raw * (1.0 / jnp.sum(raw, axis=0, keepdims=True))
        upper = scaled.astype(BF16)
        band[j, pl.ds(0, WIN), :] = upper
        band[j, pl.ds(WIN, WIN), :] = (scaled - upper.astype(F32)).astype(BF16)
        return carry

    for step in range(1, n_samp):
        copy = part_copy(step, lax.rem(samp + n_samp - step, n_samp))
        copy.wait_recv()
    summed = parts[0]
    for s in range(1, n_samp):
        summed = summed + parts[s]
    total[...] = jnp.sum(summed, axis=0, keepdims=True)
    for step in order:
        total_copy(step, me).start()
    totals[:, columns(me)] = total[...]
    for chunk in range(first, min(AHEAD, chunks)):
        send_chunk(chunk)

    @pl.when(samp < lgroups)
    def _():
        for step in order:
            load_copy(step, bin_source(step)).wait_recv()
        for step in range(1, n_samp):
            spread_copy(step, samp).start()

    lax.fori_loop(0, blocks, make_band, 0)

    land[:, pl.ds(0, EDGE)] = jnp.zeros((share, EDGE), BF16)
    land[:, pl.ds(EDGE + bins, EDGE)] = jnp.zeros((share, EDGE), BF16)
    mrows[...] = jnp.zeros(mrows.shape, BF16)

    for step in range(1, n_samp):
        owner = lax.rem(samp + n_samp - step, n_samp)

        @pl.when(owner < lgroups)
        def _(step=step, owner=owner):
            spread_copy(step, owner).wait_recv()

    for b in range(n_bin):
        for g in range(lgroups):
            lall[:, pl.ds(b * width + g * lwidth, lwidth)] = lparts[
                g, :, pl.ds(b * lwidth, lwidth)
            ]
    for copy in range(3):
        lstack[pl.ds(copy * kpad, kpad), :] = lall[...]

    for step in order:
        total_copy(step, bin_source(step)).wait_recv()
    mean_raw = totals[...] / (rows * n_samp)
    for row, value in enumerate(split3(mean_raw)):
        mrows[pl.ds(row, 1), pl.ds(EDGE, bins)] = value

    def smooth(lhs, j):
        return jnp.dot(
            jnp.concatenate([lhs, lhs], axis=1), band[j], preferred_element_type=F32
        )

    def mean_block(j, carry):
        start = pl.multiple_of(j * OUT, OUT)
        value = smooth(mrows[:, pl.ds(start, WIN)], j)
        mean[:, pl.ds(start, OUT)] = jnp.broadcast_to(
            jnp.sum(value, axis=0, keepdims=True), (8, OUT)
        )
        return carry

    lax.fori_loop(0, blocks, mean_block, 0)
    own.wait()

    def lanes(value):
        folded = value[:, 0:128]
        for k in range(1, OUT // 128):
            folded = folded + value[:, k * 128:(k + 1) * 128]
        return folded

    def finish_rows(base, size, unroll):
        rows_at = pl.ds(base, size)
        local = pl.ds(0, size)

        def smooth_block(j, carry):
            start = pl.multiple_of(j * OUT, OUT)
            value = smooth(land[rows_at, pl.ds(start, WIN)], j)
            cent[local, pl.ds(start, OUT)] = (
                value - mean[pl.ds(0, 1), pl.ds(start, OUT)]
            ).astype(BF16)
            return carry

        lax.fori_loop(0, blocks, smooth_block, 0, unroll=unroll)
        score = lax.dot_general(
            cent[local, :], lall[...], (((1,), (1,)), ((), ())), preferred_element_type=F32
        )
        scores_ref[:, rows_at] = jnp.transpose(score)[0:comps, :]
        pieces3 = jnp.concatenate(split3(score), axis=1)

        def residual_block(j, acc):
            cols = pl.ds(pl.multiple_of(j * OUT, OUT), OUT)
            value = cent[local, cols].astype(F32) - jnp.dot(
                pieces3, lstack[:, cols], preferred_element_type=F32
            )
            resid[local, cols] = value
            return acc + lanes(value)

        zero = jnp.zeros((size, 128), F32)
        acc = lax.fori_loop(0, blocks, residual_block, zero, unroll=unroll)
        row_mean = jnp.sum(acc, axis=1, keepdims=True) / bins

        def square_block(j, acc):
            cols = pl.ds(pl.multiple_of(j * OUT, OUT), OUT)
            shifted = resid[local, cols] - row_mean
            return acc + lanes(shifted * shifted)

        acc = lax.fori_loop(0, blocks, square_block, zero, unroll=unroll)
        scale = 1.0 / jnp.sqrt(jnp.sum(acc, axis=1, keepdims=True) / bins + EPS)

        def store_block(j, carry):
            cols = pl.ds(pl.multiple_of(j * OUT, OUT), OUT)
            z_ref[rows_at, cols] = ((resid[local, cols] - row_mean) * scale).astype(BF16)
            return carry

        lax.fori_loop(0, blocks, store_block, 0, unroll=unroll)

    def finish(chunk, carry):
        for step in order:
            block_copy(chunk, step, bin_source(step)).wait_recv()

        @pl.when(chunk + AHEAD < chunks - 1)
        def _():
            send_chunk(chunk + AHEAD)

        @pl.when(chunk + AHEAD == chunks - 1)
        def _():
            send_tail()

        finish_rows(pl.multiple_of(chunk * CHUNK, CHUNK), CHUNK, 2)
        return carry

    assert chunks > AHEAD
    lax.fori_loop(0, chunks - 1, finish, 0)
    for index, (offset, size) in enumerate(TAIL):
        for step in order:
            tail_copy(index, step, bin_source(step)).wait_recv()
        finish_rows(share - CHUNK + offset, size, 4)

    def drain(chunk, carry):
        for step in order:
            block_copy(chunk, step, me).wait_send()
        return carry

    lax.fori_loop(0, chunks - 1, drain, 0)
    for index in range(len(TAIL)):
        for step in order:
            tail_copy(index, step, me).wait_send()
    for step in order:
        total_copy(step, me).wait_send()

    @pl.when(samp < lgroups)
    def _():
        for step in order:
            load_copy(step, me).wait_send()
        for step in range(1, n_samp):
            spread_copy(step, samp).wait_send()

    for step in range(1, n_samp):
        part_copy(step, samp).wait_send()


def on_device(n_samp, n_bin, read_depth, gc_weight, map_weight, taps, loadings):
    rows, width = read_depth.shape
    comps = loadings.shape[0]
    share, bins = rows // n_bin, width * n_bin
    chunks, blocks = share // CHUNK, bins // OUT
    lgroups = min(n_samp, width // 128)
    kpad = -(-comps // 32) * 32
    padded = bins + 2 * EDGE
    dma = pltpu.SemaphoreType.DMA
    vmem = pl.BlockSpec(memory_space=pltpu.VMEM)
    anywhere = pl.BlockSpec(memory_space=pl.ANY)
    zscore, scores = pl.pallas_call(
        functools.partial(kernel, n_samp, n_bin),
        out_shape=(
            pltpu.VMEM((share, bins), BF16),
            pltpu.VMEM((comps, share), F32),
        ),
        in_specs=[anywhere, vmem, vmem, pl.BlockSpec(memory_space=pltpu.SMEM), vmem],
        out_specs=(vmem, vmem),
        scratch_shapes=[
            pltpu.VMEM((share, padded), BF16),
            pltpu.VMEM((2, rows // 8, width), BF16),
            pltpu.VMEM((WIN, OUT), F32),
            pltpu.VMEM((blocks, 2 * WIN, OUT), BF16),
            pltpu.VMEM((8, padded), F32),
            pltpu.VMEM((16, padded), BF16),
            pltpu.VMEM((8, bins), F32),
            pltpu.VMEM((8, width), F32),
            pltpu.VMEM((n_samp, 8, width), F32),
            pltpu.VMEM((1, width), F32),
            pltpu.VMEM((1, bins), F32),
            pltpu.VMEM((kpad, width), BF16),
            pltpu.VMEM((lgroups, kpad, width * n_bin // lgroups), BF16),
            pltpu.VMEM((kpad, bins), BF16),
            pltpu.VMEM((3 * kpad, bins), BF16),
            pltpu.VMEM((CHUNK, bins), BF16),
            pltpu.VMEM((CHUNK, bins), F32),
            dma,
            dma((8,)),
            dma((chunks, n_bin - 1)),
            dma((chunks, n_bin - 1)),
            dma((len(TAIL), n_bin - 1)),
            dma((len(TAIL), n_bin - 1)),
            dma((n_bin - 1,)),
            dma((n_bin - 1,)),
            dma((n_samp - 1,)),
            dma((n_samp - 1,)),
            dma((n_samp - 1,)),
            dma((n_samp - 1,)),
            dma((n_bin - 1,)),
            dma((n_bin - 1,)),
        ],
        compiler_params=pltpu.CompilerParams(
            collective_id=0, has_side_effects=True, vmem_limit_bytes=48 * 1024 * 1024
        ),
        name="denoise",
    )(
        read_depth, gc_weight.reshape(1, bins), map_weight.reshape(1, bins), taps, loadings
    )
    return zscore, scores.T


def solution(mesh):
    return jax.shard_map(
        functools.partial(on_device, mesh.shape["samp"], mesh.shape["bin"]),
        mesh=mesh,
        in_specs=(P("samp", "bin"), P(), P(), P(), P(None, "bin")),
        out_specs=(P(("samp", "bin"), None), P(("samp", "bin"), None)),
        check_vma=False,
    )
```

```python
import functools

import jax
import jax.numpy as jnp
from jax import lax
from jax.experimental import pallas as pl
from jax.experimental.pallas import tpu as pltpu
from jax.sharding import PartitionSpec as P

RADIUS = 16
EDGE = 128
OUT = 256
WIN = OUT + 2 * EDGE
CHUNK = 128
AHEAD = 6
TAIL = ((0, 64), (64, 32), (96, 32))
EPS = 1e-05
MESH = pl.DeviceIdType.MESH
F32 = jnp.float32
BF16 = jnp.bfloat16


def peer_order(count):
    return sorted(range(1, count), key=lambda step: (abs(2 * step - count), step))


def split3(value):
    first = value.astype(BF16)
    rest = value - first.astype(F32)
    second = rest.astype(BF16)
    third = (rest - second.astype(F32)).astype(BF16)
    return first, second, third


def kernel(
    n_samp, n_bin, x_ref, gc_ref, map_ref, taps_ref, load_ref, z_ref, scores_ref,
    land, xbuf, toeplitz, band, wpad, mrows, mean, part, parts, total, totals,
    lpad, lparts, lall, lstack, cent, resid,
    local_sem, x_sem, send_sem, recv_sem, tail_send, tail_recv, lsend, lrecv, ssend, srecv, psend, precv, tsend, trecv,
):
    rows, width = x_ref.shape
    share = rows // n_bin
    bins = width * n_bin
    chunks = share // CHUNK
    ahead = min(AHEAD, chunks - 1)
    blocks = bins // OUT
    comps = load_ref.shape[0]
    kpad = lpad.shape[0]
    lgroups = lparts.shape[0]
    lwidth = width // lgroups
    samp, me = lax.axis_index("samp"), lax.axis_index("bin")
    order = peer_order(n_bin)
    pieces = x_sem.shape[0]
    piece = rows // pieces

    def columns(index):
        return pl.ds(pl.multiple_of(index * width, width), width)

    def landed(index):
        return pl.ds(pl.multiple_of(EDGE + index * width, EDGE), width)

    own = pltpu.make_async_copy(
        x_ref.at[pl.ds(pl.multiple_of(me * share, share), share), :],
        land.at[:, landed(me)], local_sem,
    )
    slots = xbuf.shape[0]
    loads = [
        pltpu.make_async_copy(
            x_ref.at[pl.ds(p * piece, piece), :], xbuf.at[p % slots], x_sem.at[p]
        )
        for p in range(pieces)
    ]
    for copy in loads[:slots]:
        copy.start()
    own.start()

    barrier = pltpu.get_barrier_semaphore()
    for step in range(1, n_bin):
        pl.semaphore_signal(
            barrier, inc=1, device_id={"bin": lax.rem(me + step, n_bin)}, device_id_type=MESH
        )
    for step in range(1, n_samp):
        pl.semaphore_signal(
            barrier, inc=1, device_id={"samp": lax.rem(samp + step, n_samp)}, device_id_type=MESH
        )
    lpad[...] = jnp.zeros(lpad.shape, BF16)
    lpad[pl.ds(0, comps), :] = load_ref[...]

    @pl.when(samp < lgroups)
    def _():
        lparts[samp, :, pl.ds(pl.multiple_of(me * lwidth, lwidth), lwidth)] = lpad[
            :, pl.ds(pl.multiple_of(samp * lwidth, lwidth), lwidth)
        ]

    pl.semaphore_wait(barrier, n_bin + n_samp - 2)

    def load_copy(step, owner):
        return pltpu.make_async_remote_copy(
            src_ref=lpad.at[:, pl.ds(pl.multiple_of(samp * lwidth, lwidth), lwidth)],
            dst_ref=lparts.at[samp, :, pl.ds(pl.multiple_of(owner * lwidth, lwidth), lwidth)],
            send_sem=lsend.at[step - 1], recv_sem=lrecv.at[step - 1],
            device_id={"bin": lax.rem(me + step, n_bin)}, device_id_type=MESH,
        )

    def spread_copy(step, owner):
        return pltpu.make_async_remote_copy(
            src_ref=lparts.at[owner], dst_ref=lparts.at[owner],
            send_sem=ssend.at[step - 1], recv_sem=srecv.at[step - 1],
            device_id={"samp": lax.rem(samp + step, n_samp)}, device_id_type=MESH,
        )

    def block_copy(chunk, step, owner):
        to = lax.rem(me + step, n_bin)
        start = pl.multiple_of(to * share + chunk * CHUNK, CHUNK)
        return pltpu.make_async_remote_copy(
            src_ref=x_ref.at[pl.ds(start, CHUNK), :],
            dst_ref=land.at[pl.ds(pl.multiple_of(chunk * CHUNK, CHUNK), CHUNK), landed(owner)],
            send_sem=send_sem.at[chunk, step - 1], recv_sem=recv_sem.at[chunk, step - 1],
            device_id={"bin": to}, device_id_type=MESH,
        )

    def tail_copy(index, step, owner):
        to = lax.rem(me + step, n_bin)
        offset, size = TAIL[index]
        offset = offset + share - CHUNK
        start = pl.multiple_of(to * share + offset, size)
        return pltpu.make_async_remote_copy(
            src_ref=x_ref.at[pl.ds(start, size), :],
            dst_ref=land.at[pl.ds(offset, size), landed(owner)],
            send_sem=tail_send.at[index, step - 1], recv_sem=tail_recv.at[index, step - 1],
            device_id={"bin": to}, device_id_type=MESH,
        )

    def send_tail():
        for index in range(len(TAIL)):
            for step in order:
                tail_copy(index, step, me).start()

    def part_copy(step, owner):
        return pltpu.make_async_remote_copy(
            src_ref=part, dst_ref=parts.at[owner],
            send_sem=psend.at[step - 1], recv_sem=precv.at[step - 1],
            device_id={"samp": lax.rem(samp + step, n_samp)}, device_id_type=MESH,
        )

    def total_copy(step, owner):
        return pltpu.make_async_remote_copy(
            src_ref=total, dst_ref=totals.at[:, columns(owner)],
            send_sem=tsend.at[step - 1], recv_sem=trecv.at[step - 1],
            device_id={"bin": lax.rem(me + step, n_bin)}, device_id_type=MESH,
        )

    def bin_source(step):
        return lax.rem(me + n_bin - step, n_bin)

    def send_chunk(chunk):
        for step in order:
            block_copy(chunk, step, me).start()

    @pl.when(samp < lgroups)
    def _():
        for step in order:
            load_copy(step, me).start()

    first = min(2, chunks)
    for chunk in range(first):
        send_chunk(chunk)

    part[...] = jnp.zeros(part.shape, F32)
    group = 128
    for p in range(pieces):
        loads[p].wait()

        def add_rows(i, carry, p=p):
            start = pl.multiple_of(i * group, group)
            block = xbuf[p % slots, pl.ds(start, group), :].astype(F32)
            part[...] += jnp.sum(block.reshape(group // 8, 8, width), axis=0)
            return carry

        lax.fori_loop(0, piece // group, add_rows, 0)
        if p + slots < pieces:
            loads[p + slots].start()
    for step in range(1, n_samp):
        part_copy(step, samp).start()
    parts[samp] = part[...]

    wpad[...] = jnp.zeros(wpad.shape, F32)
    wpad[pl.ds(0, 1), pl.ds(EDGE, bins)] = gc_ref[...] * map_ref[...]
    toeplitz[...] = jnp.zeros(toeplitz.shape, F32)
    offset = (
        lax.broadcasted_iota(jnp.int32, (WIN, OUT), 0)
        - lax.broadcasted_iota(jnp.int32, (WIN, OUT), 1)
        - (EDGE - RADIUS)
    )

    def add_tap(tap, carry):
        toeplitz[...] = jnp.where(offset == tap, taps_ref[tap], toeplitz[...])
        return carry

    lax.fori_loop(0, 2 * RADIUS + 1, add_tap, 0)

    def make_band(j, carry):
        weight = wpad[pl.ds(0, 1), pl.ds(pl.multiple_of(j * OUT, OUT), WIN)]
        tall = jnp.transpose(jnp.broadcast_to(weight, (128, WIN)))
        raw = jnp.concatenate([tall] * (OUT // 128), axis=1) * toeplitz[...]
        scaled = raw * (1.0 / jnp.sum(raw, axis=0, keepdims=True))
        upper = scaled.astype(BF16)
        band[j, pl.ds(0, WIN), :] = upper
        band[j, pl.ds(WIN, WIN), :] = (scaled - upper.astype(F32)).astype(BF16)
        return carry

    for step in range(1, n_samp):
        copy = part_copy(step, lax.rem(samp + n_samp - step, n_samp))
        copy.wait_recv()
    summed = parts[0]
    for s in range(1, n_samp):
        summed = summed + parts[s]
    total[...] = jnp.sum(summed, axis=0, keepdims=True)
    for step in order:
        total_copy(step, me).start()
    totals[:, columns(me)] = total[...]
    for chunk in range(first, ahead):
        send_chunk(chunk)

    @pl.when(samp < lgroups)
    def _():
        for step in order:
            load_copy(step, bin_source(step)).wait_recv()
        for step in range(1, n_samp):
            spread_copy(step, samp).start()

    lax.fori_loop(0, blocks, make_band, 0)

    land[:, pl.ds(0, EDGE)] = jnp.zeros((share, EDGE), BF16)
    land[:, pl.ds(EDGE + bins, EDGE)] = jnp.zeros((share, EDGE), BF16)
    mrows[...] = jnp.zeros(mrows.shape, BF16)

    for step in range(1, n_samp):
        owner = lax.rem(samp + n_samp - step, n_samp)

        @pl.when(owner < lgroups)
        def _(step=step, owner=owner):
            spread_copy(step, owner).wait_recv()

    for b in range(n_bin):
        for g in range(lgroups):
            lall[:, pl.ds(b * width + g * lwidth, lwidth)] = lparts[
                g, :, pl.ds(b * lwidth, lwidth)
            ]
    for copy in range(3):
        lstack[pl.ds(copy * kpad, kpad), :] = lall[...]

    for step in order:
        total_copy(step, bin_source(step)).wait_recv()
    mean_raw = totals[...] / (rows * n_samp)
    for row, value in enumerate(split3(mean_raw)):
        mrows[pl.ds(row, 1), pl.ds(EDGE, bins)] = value

    def smooth(lhs, j):
        return jnp.dot(
            jnp.concatenate([lhs, lhs], axis=1), band[j], preferred_element_type=F32
        )

    def mean_block(j, carry):
        start = pl.multiple_of(j * OUT, OUT)
        value = smooth(mrows[:, pl.ds(start, WIN)], j)
        mean[:, pl.ds(start, OUT)] = jnp.broadcast_to(
            jnp.sum(value, axis=0, keepdims=True), (8, OUT)
        )
        return carry

    lax.fori_loop(0, blocks, mean_block, 0)
    own.wait()

    def lanes(value):
        folded = value[:, 0:128]
        for k in range(1, OUT // 128):
            folded = folded + value[:, k * 128:(k + 1) * 128]
        return folded

    def finish_rows(base, size, unroll):
        rows_at = pl.ds(base, size)
        local = pl.ds(0, size)

        def smooth_block(j, carry):
            start = pl.multiple_of(j * OUT, OUT)
            value = smooth(land[rows_at, pl.ds(start, WIN)], j)
            cent[local, pl.ds(start, OUT)] = (
                value - mean[pl.ds(0, 1), pl.ds(start, OUT)]
            ).astype(BF16)
            return carry

        lax.fori_loop(0, blocks, smooth_block, 0, unroll=unroll)
        score = lax.dot_general(
            cent[local, :], lall[...], (((1,), (1,)), ((), ())), preferred_element_type=F32
        )
        scores_ref[:, rows_at] = jnp.transpose(score)[0:comps, :]
        pieces3 = jnp.concatenate(split3(score), axis=1)

        def residual_block(j, acc):
            cols = pl.ds(pl.multiple_of(j * OUT, OUT), OUT)
            value = cent[local, cols].astype(F32) - jnp.dot(
                pieces3, lstack[:, cols], preferred_element_type=F32
            )
            resid[local, cols] = value
            return acc + lanes(value)

        zero = jnp.zeros((size, 128), F32)
        acc = lax.fori_loop(0, blocks, residual_block, zero, unroll=unroll)
        row_mean = jnp.sum(acc, axis=1, keepdims=True) / bins

        def square_block(j, acc):
            cols = pl.ds(pl.multiple_of(j * OUT, OUT), OUT)
            shifted = resid[local, cols] - row_mean
            return acc + lanes(shifted * shifted)

        acc = lax.fori_loop(0, blocks, square_block, zero, unroll=unroll)
        scale = 1.0 / jnp.sqrt(jnp.sum(acc, axis=1, keepdims=True) / bins + EPS)

        def store_block(j, carry):
            cols = pl.ds(pl.multiple_of(j * OUT, OUT), OUT)
            z_ref[rows_at, cols] = ((resid[local, cols] - row_mean) * scale).astype(BF16)
            return carry

        lax.fori_loop(0, blocks, store_block, 0, unroll=unroll)

    def finish(chunk, carry):
        for step in order:
            block_copy(chunk, step, bin_source(step)).wait_recv()

        @pl.when(chunk + ahead < chunks - 1)
        def _():
            send_chunk(chunk + ahead)

        @pl.when(chunk + ahead == chunks - 1)
        def _():
            send_tail()

        finish_rows(pl.multiple_of(chunk * CHUNK, CHUNK), CHUNK, 2)
        return carry

    assert ahead >= first
    lax.fori_loop(0, chunks - 1, finish, 0)
    for index, (offset, size) in enumerate(TAIL):
        for step in order:
            tail_copy(index, step, bin_source(step)).wait_recv()
        finish_rows(share - CHUNK + offset, size, 4)

    def drain(chunk, carry):
        for step in order:
            block_copy(chunk, step, me).wait_send()
        return carry

    lax.fori_loop(0, chunks - 1, drain, 0)
    for index in range(len(TAIL)):
        for step in order:
            tail_copy(index, step, me).wait_send()
    for step in order:
        total_copy(step, me).wait_send()

    @pl.when(samp < lgroups)
    def _():
        for step in order:
            load_copy(step, me).wait_send()
        for step in range(1, n_samp):
            spread_copy(step, samp).wait_send()

    for step in range(1, n_samp):
        part_copy(step, samp).wait_send()


def on_device(n_samp, n_bin, read_depth, gc_weight, map_weight, taps, loadings):
    rows, width = read_depth.shape
    comps = loadings.shape[0]
    share, bins = rows // n_bin, width * n_bin
    chunks, blocks = share // CHUNK, bins // OUT
    lgroups = min(n_samp, width // 128)
    kpad = -(-comps // 32) * 32
    padded = bins + 2 * EDGE
    dma = pltpu.SemaphoreType.DMA
    vmem = pl.BlockSpec(memory_space=pltpu.VMEM)
    anywhere = pl.BlockSpec(memory_space=pl.ANY)
    zscore, scores = pl.pallas_call(
        functools.partial(kernel, n_samp, n_bin),
        out_shape=(
            pltpu.VMEM((share, bins), BF16),
            pltpu.VMEM((comps, share), F32),
        ),
        in_specs=[anywhere, vmem, vmem, pl.BlockSpec(memory_space=pltpu.SMEM), vmem],
        out_specs=(vmem, vmem),
        scratch_shapes=[
            pltpu.VMEM((share, padded), BF16),
            pltpu.VMEM((2, rows // 8, width), BF16),
            pltpu.VMEM((WIN, OUT), F32),
            pltpu.VMEM((blocks, 2 * WIN, OUT), BF16),
            pltpu.VMEM((8, padded), F32),
            pltpu.VMEM((16, padded), BF16),
            pltpu.VMEM((8, bins), F32),
            pltpu.VMEM((8, width), F32),
            pltpu.VMEM((n_samp, 8, width), F32),
            pltpu.VMEM((1, width), F32),
            pltpu.VMEM((1, bins), F32),
            pltpu.VMEM((kpad, width), BF16),
            pltpu.VMEM((lgroups, kpad, width * n_bin // lgroups), BF16),
            pltpu.VMEM((kpad, bins), BF16),
            pltpu.VMEM((3 * kpad, bins), BF16),
            pltpu.VMEM((CHUNK, bins), BF16),
            pltpu.VMEM((CHUNK, bins), F32),
            dma,
            dma((8,)),
            dma((chunks, n_bin - 1)),
            dma((chunks, n_bin - 1)),
            dma((len(TAIL), n_bin - 1)),
            dma((len(TAIL), n_bin - 1)),
            dma((n_bin - 1,)),
            dma((n_bin - 1,)),
            dma((n_samp - 1,)),
            dma((n_samp - 1,)),
            dma((n_samp - 1,)),
            dma((n_samp - 1,)),
            dma((n_bin - 1,)),
            dma((n_bin - 1,)),
        ],
        compiler_params=pltpu.CompilerParams(
            collective_id=0, has_side_effects=True, vmem_limit_bytes=48 * 1024 * 1024
        ),
        name="denoise",
    )(
        read_depth, gc_weight.reshape(1, bins), map_weight.reshape(1, bins), taps, loadings
    )
    return zscore, scores.T


def solution(mesh):
    return jax.shard_map(
        functools.partial(on_device, mesh.shape["samp"], mesh.shape["bin"]),
        mesh=mesh,
        in_specs=(P("samp", "bin"), P(), P(), P(), P(None, "bin")),
        out_specs=(P(("samp", "bin"), None), P(("samp", "bin"), None)),
        check_vma=False,
    )
```
